32 devices in a mesh: rows: 8 (over z, x), cols: 4 (over y, core).
Axes of the slice: x: 2, y: 2, z: 4, core: 2. Of those that a mesh axis runs over, the one named last changes fastest.
Arguments:
- cube: float32 [1, 12288, 12288], P(None, 'rows', 'cols'), may hold values from -480 to 480
Outputs:
- scale_one: float32 [1, 12288, 12288], P(None, 'rows', 'cols')
- scale_two: float32 [1, 12288, 12288], P(None, 'rows', 'cols')
- scale_three: float32 [1, 12288, 12288], P(None, 'rows', 'cols')
- smooth: float32 [1, 12288, 12288], P(None, 'rows', 'cols')
- sigmas: float32 [3, 1], replicated
The draws below stay inside these ranges and needn't reach their ends.
All inputs are finite; a program needn't handle non-finite values.
Results may differ from the reference program's by a relative error of at most 0.0002.
Values sent between devices are 32-bit elements; how exact they have to be, the bound alone decides.
No kernel may reach another device: no remote copies, remote signals or barrier semaphores. Data moves between devices by JAX's collectives and lax.ppermute only.
A program may use at most 192 MiB of HBM per device.

```python
import math
import jax
import jax.numpy as jnp
from jax import lax

F = 1
NR = 12288
NC = 12288
LEVELS = 3


def profile(key, count):
    amp_key, phase_key = jax.random.split(key, 2)
    position = jnp.arange(count, dtype=jnp.float32) / (count - 1)
    freqs = jnp.array([1.0, 2.0, 3.0, 5.0, 7.0], jnp.float32)
    amps = jax.random.uniform(amp_key, (5,), jnp.float32, 0.3, 1.0)
    phases = jax.random.uniform(phase_key, (5,), jnp.float32, 0.0, 6.2831853)
    wave = jnp.sum(amps[:, None] * jnp.sin(6.2831853 * freqs[:, None] * position[None, :] + phases[:, None]), axis=0)
    wave = wave / jnp.sum(amps)
    return jnp.exp(math.log(3.0) * (0.5 * position + 0.25 * (1.0 + wave)))


def draw_cube(key, part):
    keys = jax.random.split(jax.random.fold_in(key, 11), 10)
    shape = (F, NR, NC)
    envelope = (profile(keys[4], NR)[:, None] * profile(keys[5], NC)[None, :])[None]
    block_env = (profile(keys[6], NR)[:, None] * profile(keys[7], NC)[None, :])[None]
    rough = jax.random.uniform(keys[1], shape, jnp.float32, 0.5, 1.5)
    channel = jnp.exp(jax.random.uniform(keys[2], (F, 1, 1), jnp.float32, math.log(0.5), math.log(2.0)))
    block_gain = jnp.exp(jax.random.uniform(keys[8], (F, 1, 1), jnp.float32, math.log(0.5), math.log(2.0)))
    coarse = jax.random.truncated_normal(keys[9], -4.0, 4.0, (F, NR // 4, NC // 4), jnp.float32)
    coarse = jnp.repeat(jnp.repeat(coarse, 4, axis=1), 4, axis=2)
    blocky = 0.7 * coarse * block_env * block_gain
    noise = jax.random.truncated_normal(keys[0], -4.0, 4.0, shape, jnp.float32)
    return noise * rough * envelope * channel + blocky


def setup_inputs(seed: int = 0) -> dict:
    key_of = jax.random.split(jax.random.key(seed), 2)
    cube = draw_cube(jax.random.fold_in(key_of[1], 71), 0)
    return {"cube": cube}


def filter_dim(x, dim, step):
    length = x.shape[dim]

    def part(lower, upper):
        return lax.slice_in_dim(x, lower, length - upper, axis=dim)
    outer = (part(0, 4 * step) + part(4 * step, 0)) * 0.0625
    inner = (part(step, 3 * step) + part(3 * step, step)) * 0.25
    return outer + inner + part(2 * step, 2 * step) * 0.375

def reference(cube):
    current = cube
    planes = []
    count = NR * NC
    sigma_rows = []
    for level in range(LEVELS):
        step = 2 ** level
        width = 2 * step
        padded = jnp.pad(current, ((0, 0), (width, width), (width, width)), mode='reflect')
        nextsmooth = filter_dim(filter_dim(padded, 1, step), 2, step)
        plane = current - nextsmooth
        planes.append(plane)
        squares = lax.optimization_barrier(jnp.sum(plane * plane, axis=(1, 2)))
        sigma_rows.append(jnp.sqrt(squares / count + 1e-06))
        current = nextsmooth
    return (planes[0], planes[1], planes[2], current, jnp.stack(sigma_rows))
```

```python
import functools

import jax
import jax.numpy as jnp
from jax import lax
from jax.experimental import pallas as pl
from jax.experimental.pallas import tpu as pltpu
from jax.sharding import PartitionSpec as P

LANES = 128
TILE = 128
REACH = 14
TOP = 24
HEAD = 16
SIDE = 8
LAG = dict(a=0, b=1, c=2, d=2, e=2, f=3)
SKEW = dict(a=0, b=1, c=2, d=4, e=6, f=7)


def five(load, step):
    a, b, c, d, e = (load(k * step) for k in (-2, -1, 0, 1, 2))
    return (a + e) + 4.0 * (b + d) + 6.0 * c


def kernel(x, top, bottom, sides, w1, w2, w3, smooth, squares, xs, y1t, c1t, c1, z, c2, y3t, o1, o2, o3, o4, acc, isem, osem,
           *, rows, strips):
    tiles = (rows + 2 * HEAD + TILE - 1) // TILE
    outs = ((o1, w1, "b"), (o2, w2, "d"), (o3, w3, "f"), (o4, smooth, "f"))

    def in_copies(strip, slot):
        cols = pl.ds(pl.multiple_of(strip * LANES, LANES), LANES)
        return (
            pltpu.make_async_copy(x.at[:, cols], xs.at[slot, pl.ds(TOP, rows), :], isem.at[slot, 0]),
            pltpu.make_async_copy(top.at[:, cols], xs.at[slot, pl.ds(0, TOP), :], isem.at[slot, 1]),
            pltpu.make_async_copy(bottom.at[:, cols], xs.at[slot, pl.ds(TOP + rows, TOP), :], isem.at[slot, 2]),
        )

    def side_copy(side, slot):
        return pltpu.make_async_copy(sides.at[side], xs.at[slot, pl.ds(0, rows + 2 * TOP), :], isem.at[slot, 0])

    def fetch(s, wait):
        slot = lax.rem(s, 5)
        for side, at in ((0, 0), (1, strips + 1)):

            @pl.when(s == at)
            def _():
                c = side_copy(side, slot)
                c.wait() if wait else c.start()

        @pl.when((s >= 1) & (s <= strips))
        def _():
            for c in in_copies(s - 1, slot):
                c.wait() if wait else c.start()

    def out_copy(k, s):
        buf, dst, _ = outs[k]
        slot = lax.rem(s, 3)
        cols = pl.ds(pl.multiple_of((s - 1) * LANES, LANES), LANES)
        return pltpu.make_async_copy(buf.at[slot, pl.ds(HEAD, rows), :], dst.at[:, cols], osem.at[k, slot])

    def boundary(big):
        fetch(big, True)
        fetch(big + 2, False)
        for k, (_, _, st) in enumerate(outs):
            done = big - LAG[st] - 2

            @pl.when((done - 1 >= 1) & (done - 1 <= strips))
            def _():
                out_copy(k, done - 1).wait()

            @pl.when((done >= 1) & (done <= strips))
            def _():
                out_copy(k, done).start()

    def place(st, big, r):
        q = r - SKEW[st]
        behind = q < 0
        rb = jnp.where(behind, q + tiles, q)
        s = big - LAG[st] - jnp.where(behind, 1, 0)
        return s, rb

    def ring(s, n):
        return lax.rem(s + 2 * n, n)

    def put(buf, s, rb, value):
        buf[ring(s, 3), rb, pl.ds(SIDE, LANES), :] = value
        buf[ring(s + 1, 3), rb, pl.ds(0, SIDE), :] = value[LANES - SIDE :]
        buf[ring(s - 1, 3), rb, pl.ds(SIDE + LANES, SIDE), :] = value[:SIDE]

    def add_squares(k, s, rb, plane):
        sq = (plane * plane).reshape(TILE // 8, 8, LANES)
        cut = HEAD // 8
        ok = (s >= 1) & (s <= strips)
        zero = jnp.zeros((8, LANES), jnp.float32)
        first = jnp.where(ok & (rb > 0), jnp.sum(sq[:cut], axis=0), zero)
        rest = jnp.where(ok & (rb < tiles - 1), jnp.sum(sq[cut:], axis=0), zero)
        acc[k] += first + rest

    def nat(buf, n, s, rb, shift=0):
        return buf[ring(s, n), pl.ds(pl.multiple_of(rb * TILE, TILE) + (TOP - HEAD) + shift, TILE), :]

    def nat_put(buf, n, s, rb, value):
        buf[ring(s, n), pl.ds(pl.multiple_of(rb * TILE, TILE) + (TOP - HEAD), TILE), :] = value

    def out_put(buf, s, rb, value):
        buf[ring(s, 3), pl.ds(pl.multiple_of(rb * TILE, TILE), TILE), :] = value

    def stage_a(s, rb):
        put(y1t, s, rb, five(lambda k: nat(xs, 5, s, rb, k), 1).T)

    def columns(buf, s, rb, step):
        return five(lambda k: buf[ring(s, 3), rb, pl.ds(SIDE + k, LANES), :], step)

    def stage_b(s, rb):
        value = columns(y1t, s, rb, 1) * (1.0 / 256)
        put(c1t, s, rb, value)
        value = value.T
        nat_put(c1, 3, s, rb, value)
        plane = nat(xs, 5, s, rb) - value
        out_put(o1, s, rb, plane)
        add_squares(0, s, rb, plane)

    def stage_c(s, rb):
        nat_put(z, 2, s, rb, columns(c1t, s, rb, 2).T)

    def stage_d(s, rb):
        value = five(lambda k: nat(z, 2, s, rb, k), 2) * (1.0 / 256)
        nat_put(c2, 3, s, rb, value)
        plane = nat(c1, 3, s, rb) - value
        out_put(o2, s, rb, plane)
        add_squares(1, s, rb, plane)

    def stage_e(s, rb):
        put(y3t, s, rb, five(lambda k: nat(c2, 3, s, rb, k), 4).T)

    def stage_f(s, rb):
        value = (columns(y3t, s, rb, 4) * (1.0 / 256)).T
        out_put(o4, s, rb, value)
        plane = nat(c2, 3, s, rb) - value
        out_put(o3, s, rb, plane)
        add_squares(2, s, rb, plane)

    stages = dict(a=stage_a, b=stage_b, c=stage_c, d=stage_d, e=stage_e, f=stage_f)

    def run(first, last, names, count=None):
        def outer(big, carry):
            boundary(big)

            def inner(r, c):
                for name in reversed(names):
                    stages[name](*place(name, big, r))
                return c

            return lax.fori_loop(0, tiles if count is None else count, inner, carry)

        lax.fori_loop(first, last, outer, 0)

    acc[...] = jnp.zeros_like(acc)
    fetch(jnp.int32(0), False)
    fetch(jnp.int32(1), False)
    run(0, 1, "a")
    run(1, 2, "ab")
    run(2, 4, "abcde")
    run(4, strips + 2, "abcdef")
    run(strips + 2, strips + 4, "bcdef")
    run(strips + 4, strips + 5, "cdef", SKEW["f"])
    boundary(jnp.int32(strips + 5))
    boundary(jnp.int32(strips + 6))
    squares[...] = acc[...]


def transform(x, top, bottom, sides):
    rows, cols = x.shape
    strips = cols // LANES
    assert rows % TILE == 0
    tiles = (rows + 2 * HEAD + TILE - 1) // TILE
    tall = tiles * TILE + 2 * (TOP - HEAD)
    hbm = pl.BlockSpec(memory_space=pl.ANY)
    vmem = pl.BlockSpec(memory_space=pltpu.VMEM)
    big = jax.ShapeDtypeStruct((rows, cols), jnp.float32)
    natural = lambda n: pltpu.VMEM((n, tall, LANES), jnp.float32)
    turned = pltpu.VMEM((3, tiles, LANES + 2 * SIDE, TILE), jnp.float32)
    out = pltpu.VMEM((3, tiles * TILE, LANES), jnp.float32)
    return pl.pallas_call(
        functools.partial(kernel, rows=rows, strips=strips),
        in_specs=[hbm, hbm, hbm, hbm],
        out_specs=[hbm, hbm, hbm, hbm, vmem],
        out_shape=[big, big, big, big, jax.ShapeDtypeStruct((3, 8, LANES), jnp.float32)],
        scratch_shapes=[
            natural(5), turned, turned, natural(3), natural(2), natural(3), turned, out, out, out, out,
            pltpu.VMEM((3, 8, LANES), jnp.float32),
            pltpu.SemaphoreType.DMA((5, 3)),
            pltpu.SemaphoreType.DMA((4, 3)),
        ],
        compiler_params=pltpu.CompilerParams(vmem_limit_bytes=56 * 1024 * 1024),
        name="starlet",
    )(x, top, bottom, sides)


def neighbours(first, last, axis):
    count = lax.axis_size(axis)
    up = [(i, i + 1) for i in range(count - 1)]
    down = [(i + 1, i) for i in range(count - 1)]
    return lax.ppermute(last, axis, up), lax.ppermute(first, axis, down)


def halo(x, axis, dim):
    length = x.shape[dim]
    take = lambda a, b: lax.slice_in_dim(x, a, b, axis=dim)
    before, after = neighbours(take(0, REACH), take(length - REACH, length), axis)
    pos, count = lax.axis_index(axis), lax.axis_size(axis)
    before = jnp.where(pos == 0, jnp.flip(take(1, REACH + 1), dim), before)
    after = jnp.where(pos == count - 1, jnp.flip(take(length - REACH - 1, length - 1), dim), after)
    return before, after


def total(value):
    for axis in ("cols", "rows"):
        size = lax.axis_size(axis)
        hop = 1
        while hop < size:
            value = value + lax.ppermute(value, axis, [(i, i ^ hop) for i in range(size)])
            hop *= 2
    return value


def on_device(cube):
    x = cube[0]
    rows, cols = x.shape
    above, below = halo(x, "rows", 0)
    edge = lambda a, b: jnp.concatenate([above[:, a:b], x[:, a:b], below[:, a:b]], axis=0)
    first, last = edge(0, REACH + 1), edge(cols - REACH - 1, cols)
    left, right = neighbours(first[:, :REACH], last[:, 1:], "cols")
    pos, count = lax.axis_index("cols"), lax.axis_size("cols")
    left = jnp.where(pos == 0, jnp.flip(first[:, 1:], 1), left)
    right = jnp.where(pos == count - 1, jnp.flip(last[:, :REACH], 1), right)
    extra = TOP - REACH
    top = jnp.pad(above, ((extra, 0), (0, 0)))
    bottom = jnp.pad(below, ((0, extra), (0, 0)))
    sides = jnp.stack([
        jnp.pad(left, ((extra, extra), (LANES - REACH, 0))),
        jnp.pad(right, ((extra, extra), (0, LANES - REACH))),
    ])
    w1, w2, w3, smooth, squares = transform(x, top, bottom, sides)
    pixels = float(lax.axis_size("rows") * lax.axis_size("cols") * rows * cols)
    sums = total(jnp.sum(squares, axis=(1, 2)))
    sigmas = jnp.sqrt(sums / pixels + 1e-06)[:, None]
    return w1[None], w2[None], w3[None], smooth[None], sigmas


def solution(mesh):
    whole = P(None, "rows", "cols")
    return jax.shard_map(
        on_device, mesh=mesh, in_specs=(whole,), out_specs=(whole, whole, whole, whole, P()), check_vma=False
    )
```

```python
import functools

import jax
import jax.numpy as jnp
from jax import lax
from jax.experimental import pallas as pl
from jax.experimental.pallas import tpu as pltpu
from jax.sharding import PartitionSpec as P

LANES = 128
TILE = 128
REACH = 14
EDGE = 16
HEAD = 24
PAD = 8
SIDE = 8
RING = 4
LONG = 6


def five(load, step):
    a, b, c, d, e = (load(k * step) for k in (-2, -1, 0, 1, 2))
    return (a + e) + 4.0 * (b + d) + 6.0 * c


STAGES = "aAbBcCdeEfF"


def stage_lags(tiles):
    even = lambda n: n + n % 2
    lags = dict(a=0)
    after = dict(A=0, b=tiles, B=0, c=tiles, C=0, d=1, e=1, E=0, f=tiles, F=0)
    source = dict(A="a", b="A", B="b", c="b", C="c", d="C", e="d", E="e", f="E", F="f")
    for st in STAGES[1:]:
        lags[st] = even(lags[source[st]] + after[st] + 2)
    return lags


def kernel(x, top, bottom, left, right, first, last, w1, w2, w3, smooth, squares, xs, y1t, c1t, c1, z, c2, y3t, o1, o2, o3, o4,
           ya, zt, ye, c3t, acc, edge, isem, osem, *, rows, strips):
    tiles = (rows + HEAD + EDGE + TILE - 1) // TILE
    tall = tiles * TILE
    lags = stage_lags(tiles)
    ring, long = RING * tiles, LONG * tiles
    outs = ((o1, w1, "B"), (o2, w2, "d"), (o3, w3, "F"), (o4, smooth, "F"))

    def slot_of(s):
        return lax.rem(s, LONG)

    def in_copies(s):
        slot = slot_of(s)
        base = pl.multiple_of(slot * tall + PAD, 8)
        cols = pl.ds(pl.multiple_of((s - 1) * LANES, LANES), LANES)
        return (
            pltpu.make_async_copy(x.at[:, cols], xs.at[pl.ds(base + HEAD, rows), :], isem.at[slot, 0]),
            pltpu.make_async_copy(top.at[:, cols], xs.at[pl.ds(base + HEAD - EDGE, EDGE), :], isem.at[slot, 1]),
            pltpu.make_async_copy(bottom.at[:, cols], xs.at[pl.ds(base + HEAD + rows, EDGE), :], isem.at[slot, 2]),
        )

    row_pos, col_pos = lax.axis_index("rows"), lax.axis_index("cols")
    row_ends = (row_pos == 0, row_pos == lax.axis_size("rows") - 1)
    col_ends = (col_pos == 0, col_pos == lax.axis_size("cols") - 1)

    def build_side(side, s):
        got, own = ((left, first), (right, last))[side]

        edge[...] = got[...]

        @pl.when(col_ends[side])
        def _():
            for k in range(1, EDGE):
                to = EDGE - k if side == 0 else k - 1
                edge[pl.ds(to, 1), :] = own[pl.ds(k if side == 0 else EDGE - 1 - k, 1), :]

        base = pl.multiple_of(slot_of(s) * tall + PAD, 8)
        blank = jnp.zeros((LANES - EDGE, TILE), jnp.float32)

        def one(rb, c):
            at = pl.multiple_of(rb * TILE, TILE)
            part = edge[:, pl.ds(at, TILE)]
            part = jnp.concatenate([blank, part] if side == 0 else [part, blank], axis=0)
            xs[pl.ds(base + at, TILE), :] = part.T
            return c

        lax.fori_loop(0, tiles, one, 0)

    def mirror_rows(s):
        base = slot_of(s) * tall + PAD + HEAD

        @pl.when(row_ends[0])
        def _():
            for k in range(1, REACH + 1):
                xs[pl.ds(base - k, 1), :] = xs[pl.ds(base + k, 1), :]

        @pl.when(row_ends[1])
        def _():
            for k in range(1, REACH + 1):
                xs[pl.ds(base + rows - 1 + k, 1), :] = xs[pl.ds(base + rows - 1 - k, 1), :]

    def request(s):
        @pl.when((s >= 1) & (s <= strips))
        def _():
            for c in in_copies(s):
                c.start()

    def receive(s):
        for side, at in ((0, 0), (1, strips + 1)):

            @pl.when(s == at)
            def _():
                build_side(side, s)

        @pl.when((s >= 1) & (s <= strips))
        def _():
            for c in in_copies(s):
                c.wait()

        @pl.when(s <= strips + 1)
        def _():
            mirror_rows(s)

    def out_copy(k, s):
        buf, dst, _ = outs[k]
        slot = slot_of(s)
        base = pl.multiple_of(slot * tall + HEAD, 8)
        cols = pl.ds(pl.multiple_of((s - 1) * LANES, LANES), LANES)
        return pltpu.make_async_copy(buf.at[pl.ds(base, rows), :], dst.at[:, cols], osem.at[k, slot])

    def boundary(p):
        for u in (0, 1):
            request(2 * p + 2 + u)
        for u in (0, 1):
            receive(2 * p + u)
        for k, (_, _, st) in enumerate(outs):
            newest = 2 * p - 1 - -(-lags[st] // tiles)
            for s in (newest - 3, newest - 2):

                @pl.when((s >= 1) & (s <= strips))
                def _():
                    out_copy(k, s).wait()

            for s in (newest - 1, newest):

                @pl.when((s >= 1) & (s <= strips))
                def _():
                    out_copy(k, s).start()

    def wrap(i, n):
        return jnp.where(i < 0, i + n, i)

    class Place:
        def __init__(self, st, p, r, m, ml):
            lag = lags[st]
            self.short = wrap(m - lag % ring, ring)
            self.long = wrap(ml - lag % long, long)
            self.q = 2 * tiles * p + 2 * r - lag
            self.x = 2 * r + (-lag) % tiles

        def rows_at(self, u, buf_long=False):
            i = self.long if buf_long else self.short
            return pl.multiple_of(i * TILE, TILE) + u * TILE

        def turned_at(self, u, strip=0):
            if strip == 0:
                return pl.multiple_of(self.short * (LANES + 2 * SIDE), 8) + u * (LANES + 2 * SIDE)
            i = self.short + u + strip * tiles
            i = jnp.where(i >= ring, i - ring, i) if strip > 0 else wrap(i, ring)
            return pl.multiple_of(i * (LANES + 2 * SIDE), 8)

        def masks(self, u):
            q, rb = self.q + u, self.x + u
            for _ in range(3):
                rb = jnp.where(rb >= tiles, rb - tiles, rb)
            ok = (q >= tiles) & (q < tiles * (strips + 1))
            return ok & (rb > 0), ok & (rb < tiles - 1)

    def nat(buf, at, u, shift=0, is_long=False):
        return buf[pl.ds(at.rows_at(u, is_long) + PAD + shift, TILE), :]

    def nat_put(buf, at, u, value):
        buf[pl.ds(at.rows_at(u) + PAD, TILE), :] = value

    def out_put(buf, at, u, value):
        buf[pl.ds(at.rows_at(u, True), TILE), :] = value

    def put(buf, at, u, value):
        buf[pl.ds(at.turned_at(u) + SIDE, LANES), :] = value
        buf[pl.ds(at.turned_at(u, 1), SIDE), :] = value[LANES - SIDE :]
        buf[pl.ds(at.turned_at(u, -1) + SIDE + LANES, SIDE), :] = value[:SIDE]

    def columns(buf, at, u, step):
        return five(lambda k: buf[pl.ds(at.turned_at(u) + SIDE + k, LANES), :], step)

    def add_squares(k, at, u, plane):
        sq = (plane * plane).reshape(TILE // 8, 8, LANES)
        cut = HEAD // 8
        first_ok, rest_ok = at.masks(u)
        zero = jnp.zeros((8, LANES), jnp.float32)
        first = jnp.where(first_ok, jnp.sum(sq[:cut], axis=0), zero)
        rest = jnp.where(rest_ok, jnp.sum(sq[cut:], axis=0), zero)
        acc[k] += first + rest

    def hold(buf, u, value):
        buf[pl.ds(u * TILE, TILE), :] = value

    def held(buf, u):
        return buf[pl.ds(u * TILE, TILE), :].T

    def rows_a(at, u):
        hold(ya, u, five(lambda k: nat(xs, at, u, k, True), 1))

    def turn_a(at, u):
        put(y1t, at, u, held(ya, u))

    def cols_b(at, u):
        put(c1t, at, u, columns(y1t, at, u, 1) * (1.0 / 256))

    def turn_b(at, u):
        value = c1t[pl.ds(at.turned_at(u) + SIDE, LANES), :].T
        nat_put(c1, at, u, value)
        plane = nat(xs, at, u, 0, True) - value
        out_put(o1, at, u, plane)
        add_squares(0, at, u, plane)

    def cols_c(at, u):
        hold(zt, u, columns(c1t, at, u, 2))

    def turn_c(at, u):
        nat_put(z, at, u, held(zt, u))

    def rows_d(at, u):
        value = five(lambda k: nat(z, at, u, k), 2) * (1.0 / 256)
        nat_put(c2, at, u, value)
        plane = nat(c1, at, u) - value
        out_put(o2, at, u, plane)
        add_squares(1, at, u, plane)

    def rows_e(at, u):
        hold(ye, u, five(lambda k: nat(c2, at, u, k), 4))

    def turn_e(at, u):
        put(y3t, at, u, held(ye, u))

    def cols_f(at, u):
        hold(c3t, u, columns(y3t, at, u, 4) * (1.0 / 256))

    def turn_f(at, u):
        value = held(c3t, u)
        out_put(o4, at, u, value)
        plane = nat(c2, at, u) - value
        out_put(o3, at, u, plane)
        add_squares(2, at, u, plane)

    stages = dict(
        a=rows_a, A=turn_a, b=cols_b, B=turn_b, c=cols_c, C=turn_c, d=rows_d, e=rows_e, E=turn_e, f=cols_f, F=turn_f
    )

    def run(spans):
        def outer(p, carry):
            boundary(p)
            for lo, hi, names in spans:

                def inner(r, c, names=names):
                    m, ml = c
                    for name in reversed(names):
                        at = Place(name, p, r, m, ml)
                        for u in (0, 1):
                            stages[name](at, u)
                    m, ml = m + 2, ml + 2
                    return jnp.where(m >= ring, m - ring, m), jnp.where(ml >= long, ml - long, ml)

                carry = lax.fori_loop(lo, hi, inner, carry)
            return carry

        return outer

    acc[...] = jnp.zeros_like(acc)
    for u in (0, 1):
        request(jnp.int32(u))
    ends = {st: tiles * (strips + 2) + lag for st, lag in lags.items()}
    for st in "fF":
        ends[st] -= tiles
    starts = dict(lags, f=lags["f"] + tiles, F=lags["F"] + tiles)
    carry = (jnp.int32(0), jnp.int32(0))
    total = -(-ends["F"] // (2 * tiles))
    plan = []
    for p in range(total):
        spans = []
        for r in range(tiles):
            i = 2 * (tiles * p + r)
            names = "".join(st for st in STAGES if starts[st] - 1 <= i < ends[st])
            if spans and (spans[-1][2] == names or spans[-1][1] - spans[-1][0] < 2):
                names = "".join(st for st in STAGES if st in names or st in spans[-1][2])
                spans[-1] = (spans[-1][0], r + 1, names)
            elif names:
                spans.append((r, r + 1, names))
        if plan and plan[-1][2] == spans:
            plan[-1] = (plan[-1][0], p + 1, spans)
        else:
            plan.append((p, p + 1, spans))
    for lo, hi, spans in plan:
        carry = lax.fori_loop(lo, hi, run(spans), carry)
    for p in range(total, total + 4):
        boundary(jnp.int32(p))
    lane = lax.broadcasted_iota(jnp.int32, (1, LANES), 1)
    sums = jnp.zeros((1, LANES), jnp.float32)
    for k in range(3):
        sums = jnp.where(lane == k, jnp.sum(acc[k]), sums)
    squares[...] = jnp.broadcast_to(sums[None], squares.shape)


def transform(x, top, bottom, left, right, first, last, devices):
    rows, cols = x.shape
    strips = cols // LANES
    assert rows % TILE == 0 and cols % (2 * LANES) == 0
    tiles = (rows + HEAD + EDGE + TILE - 1) // TILE
    hbm = pl.BlockSpec(memory_space=pl.ANY)
    vmem = pl.BlockSpec(memory_space=pltpu.VMEM)
    big = jax.ShapeDtypeStruct((rows, cols), jnp.float32)
    natural = lambda n: pltpu.VMEM((n * tiles * TILE + 2 * PAD, LANES), jnp.float32)
    turned = pltpu.VMEM((RING * tiles * (LANES + 2 * SIDE), TILE), jnp.float32)
    held = pltpu.VMEM((2 * TILE, LANES), jnp.float32)
    out = pltpu.VMEM((LONG * tiles * TILE, LANES), jnp.float32)
    return pl.pallas_call(
        functools.partial(kernel, rows=rows, strips=strips),
        in_specs=[hbm, hbm, hbm, vmem, vmem, vmem, vmem],
        out_specs=[hbm, hbm, hbm, hbm, vmem],
        out_shape=[big, big, big, big, jax.ShapeDtypeStruct((devices, 1, LANES), jnp.float32)],
        scratch_shapes=[
            natural(LONG), turned, turned, natural(RING), natural(RING), natural(RING), turned, out, out, out, out,
            held, held, held, held,
            pltpu.VMEM((3, 8, LANES), jnp.float32),
            pltpu.VMEM((EDGE, tiles * TILE), jnp.float32),
            pltpu.SemaphoreType.DMA((LONG, 3)),
            pltpu.SemaphoreType.DMA((4, LONG)),
        ],
        compiler_params=pltpu.CompilerParams(vmem_limit_bytes=58 * 1024 * 1024),
        name="starlet",
    )(x, top, bottom, left, right, first, last)


def edge_kernel(left, right, first, last):
    for at in range(0, left.shape[0], TILE):
        first[:, at : at + TILE] = left[at : at + TILE, :].T[:EDGE]
        last[:, at : at + TILE] = right[at : at + TILE, :].T[LANES - EDGE :]


def turned_edges(x):
    rows, cols = x.shape
    strip = lambda i: pl.BlockSpec((rows, LANES), lambda g: (0, i))
    out = pl.BlockSpec((EDGE, rows), lambda g: (0, 0))
    shape = jax.ShapeDtypeStruct((EDGE, rows), jnp.float32)
    return pl.pallas_call(
        edge_kernel,
        grid=(1,),
        in_specs=[strip(0), strip(cols // LANES - 1)],
        out_specs=[out, out],
        out_shape=[shape, shape],
        cost_estimate=pl.CostEstimate(flops=0, bytes_accessed=8 * rows * LANES, transcendentals=0),
        name="edges",
    )(x, x)


def neighbours(first, last, axis):
    count = lax.axis_size(axis)
    up = [(i, i + 1) for i in range(count - 1)]
    down = [(i + 1, i) for i in range(count - 1)]
    return lax.ppermute(last, axis, up), lax.ppermute(first, axis, down)


def on_device(cube):
    x = cube[0]
    rows, cols = x.shape
    devices = lax.axis_size("rows") * lax.axis_size("cols")
    tall = (rows + HEAD + EDGE + TILE - 1) // TILE * TILE
    above, below = neighbours(x[:EDGE], x[rows - EDGE :], "rows")

    inner = turned_edges(x)

    def edge(mid, a, b):
        parts = [above[:, a:b].T, mid, below[:, a:b].T]
        return jnp.pad(jnp.concatenate(parts, axis=1), ((0, 0), (HEAD - EDGE, tall - rows - HEAD - EDGE)))

    first, last = edge(inner[0], 0, EDGE), edge(inner[1], cols - EDGE, cols)
    left, right = neighbours(first, last, "cols")
    w1, w2, w3, smooth, squares = transform(x, above, below, left, right, first, last, devices)
    sums = jnp.sum(lax.all_to_all(squares, ("rows", "cols"), 0, 0), axis=(0, 1))
    sigmas = jnp.sqrt(sums[:3] / float(devices * rows * cols) + 1e-06)[:, None]
    return w1[None], w2[None], w3[None], smooth[None], sigmas


def solution(mesh):
    whole = P(None, "rows", "cols")
    return jax.shard_map(
        on_device, mesh=mesh, in_specs=(whole,), out_specs=(whole, whole, whole, whole, P()), check_vma=False
    )
```

```python
import functools

import jax
import jax.numpy as jnp
from jax import lax
from jax.experimental import pallas as pl
from jax.experimental.pallas import tpu as pltpu
from jax.sharding import PartitionSpec as P

LANES = 128
TILE = 128
REACH = 14
EDGE = 16
HEAD = 24
PAD = 8
SIDE = 8
RING = 4
LONG = 6


def five(load, step):
    a, b, c, d, e = (load(k * step) for k in (-2, -1, 0, 1, 2))
    return (a + e) + 4.0 * (b + d) + 6.0 * c


STAGES = "aAbBcCdeEfF"


def stage_lags(tiles):
    even = lambda n: n + n % 2
    lags = dict(a=0)
    after = dict(A=0, b=tiles, B=0, c=tiles, C=0, d=1, e=1, E=0, f=tiles, F=0)
    source = dict(A="a", b="A", B="b", c="b", C="c", d="C", e="d", E="e", f="E", F="f")
    for st in STAGES[1:]:
        lags[st] = even(lags[source[st]] + after[st] + 2)
    return lags


def kernel(x, top, bottom, left, right, first, last, w1, w2, w3, smooth, squares, xs, y1t, c1t, c1, z, c2, y3t, o1, o2, o3, o4,
           ya, zt, ye, c3t, acc, edge, isem, osem, *, rows, strips):
    tiles = (rows + HEAD + EDGE + TILE - 1) // TILE
    tall = tiles * TILE
    lags = stage_lags(tiles)
    ring, long = RING * tiles, LONG * tiles
    outs = ((o1, w1, "B"), (o2, w2, "d"), (o3, w3, "F"), (o4, smooth, "F"))

    def slot_of(s):
        return lax.rem(s, LONG)

    def in_copies(s):
        slot = slot_of(s)
        base = pl.multiple_of(slot * tall + PAD, 8)
        cols = pl.ds(pl.multiple_of((s - 1) * LANES, LANES), LANES)
        return (
            pltpu.make_async_copy(x.at[:, cols], xs.at[pl.ds(base + HEAD, rows), :], isem.at[slot, 0]),
            pltpu.make_async_copy(top.at[:, cols], xs.at[pl.ds(base + HEAD - EDGE, EDGE), :], isem.at[slot, 1]),
            pltpu.make_async_copy(bottom.at[:, cols], xs.at[pl.ds(base + HEAD + rows, EDGE), :], isem.at[slot, 2]),
        )

    row_pos, col_pos = lax.axis_index("rows"), lax.axis_index("cols")
    row_ends = (row_pos == 0, row_pos == lax.axis_size("rows") - 1)
    col_ends = (col_pos == 0, col_pos == lax.axis_size("cols") - 1)

    def build_side(side, s):
        got, own = ((left, first), (right, last))[side]
        edge[...] = got[...]

        @pl.when(col_ends[side])
        def _():
            for k in range(1, EDGE):
                at = EDGE - k if side == 0 else k - 1
                edge[pl.ds(at, 1), :] = own[pl.ds(k if side == 0 else EDGE - 1 - k, 1), :]

        base = pl.multiple_of(slot_of(s) * tall + PAD + HEAD, 8)
        blank = jnp.zeros((LANES - EDGE, TILE), jnp.float32)

        def turn(part):
            return jnp.concatenate([blank, part] if side == 0 else [part, blank], axis=0).T

        for at in range(0, rows, TILE):
            xs[pl.ds(base + at, TILE), :] = turn(edge[:, at : at + TILE])
        ends = turn(edge[:, rows:])
        xs[pl.ds(base - EDGE, EDGE), :] = ends[:EDGE]
        xs[pl.ds(base + rows, EDGE), :] = ends[EDGE : 2 * EDGE]

    def mirror_rows(s):
        base = slot_of(s) * tall + PAD + HEAD

        @pl.when(row_ends[0])
        def _():
            for k in range(1, REACH + 1):
                xs[pl.ds(base - k, 1), :] = xs[pl.ds(base + k, 1), :]

        @pl.when(row_ends[1])
        def _():
            for k in range(1, REACH + 1):
                xs[pl.ds(base + rows - 1 + k, 1), :] = xs[pl.ds(base + rows - 1 - k, 1), :]

    def guarded(fn, p, span, ahead):
        lo, hi = 2 * span[0] + ahead, 2 * (span[1] - 1) + ahead
        s = 2 * p + ahead
        if lo >= 1 and hi <= strips:
            fn(s)
        elif hi >= 1 and lo <= strips:
            pl.when((s >= 1) & (s <= strips))(lambda: fn(s))

    def request(s):
        for c in in_copies(s):
            c.start()

    def receive(s):
        for c in in_copies(s):
            c.wait()
        mirror_rows(s)

    def out_copy(k, s):
        buf, dst, _ = outs[k]
        slot = slot_of(s)
        base = pl.multiple_of(slot * tall + HEAD, 8)
        cols = pl.ds(pl.multiple_of((s - 1) * LANES, LANES), LANES)
        return pltpu.make_async_copy(buf.at[pl.ds(base, rows), :], dst.at[:, cols], osem.at[k, slot])

    def boundary(p, span):
        for u in (2, 3):
            guarded(request, p, span, u)
        for u in (0, 1):
            guarded(receive, p, span, u)
        if span[0] <= strips // 2 < span[1]:

            @pl.when(p == strips // 2)
            def _():
                build_side(1, strips + 1)
                mirror_rows(strips + 1)

        for k, (_, _, st) in enumerate(outs):
            newest = -1 - -(-lags[st] // tiles)
            for ahead in (newest - 3, newest - 2):
                guarded(lambda s: out_copy(k, s).wait(), p, span, ahead)
            for ahead in (newest - 1, newest):
                guarded(lambda s: out_copy(k, s).start(), p, span, ahead)

    def wrap(i, n):
        return jnp.where(i < 0, i + n, i)

    class Place:
        def __init__(self, st, p, r, m, ml):
            lag = lags[st]
            self.short = wrap(m - lag % ring, ring)
            self.long = wrap(ml - lag % long, long)
            self.q = 2 * tiles * p + 2 * r - lag
            self.x = 2 * r + (-lag) % tiles

        def rows_at(self, u, buf_long=False):
            i = self.long if buf_long else self.short
            return pl.multiple_of(i * TILE, TILE) + u * TILE

        def turned_at(self, u, strip=0):
            if strip == 0:
                return pl.multiple_of(self.short * (LANES + 2 * SIDE), 8) + u * (LANES + 2 * SIDE)
            i = self.short + u + strip * tiles
            i = jnp.where(i >= ring, i - ring, i) if strip > 0 else wrap(i, ring)
            return pl.multiple_of(i * (LANES + 2 * SIDE), 8)

        def masks(self, u):
            q, rb = self.q + u, self.x + u
            for _ in range(3):
                rb = jnp.where(rb >= tiles, rb - tiles, rb)
            ok = (q >= tiles) & (q < tiles * (strips + 1))
            return ok & (rb > 0), ok & (rb < tiles - 1)

    def nat(buf, at, u, shift=0, is_long=False):
        return buf[pl.ds(at.rows_at(u, is_long) + PAD + shift, TILE), :]

    def nat_put(buf, at, u, value):
        buf[pl.ds(at.rows_at(u) + PAD, TILE), :] = value

    def out_put(buf, at, u, value):
        buf[pl.ds(at.rows_at(u, True), TILE), :] = value

    def put(buf, at, u, value):
        buf[pl.ds(at.turned_at(u) + SIDE, LANES), :] = value
        buf[pl.ds(at.turned_at(u, 1), SIDE), :] = value[LANES - SIDE :]
        buf[pl.ds(at.turned_at(u, -1) + SIDE + LANES, SIDE), :] = value[:SIDE]

    def columns(buf, at, u, step):
        return five(lambda k: buf[pl.ds(at.turned_at(u) + SIDE + k, LANES), :], step)

    def add_squares(k, at, u, plane):
        sq = (plane * plane).reshape(TILE // 8, 8, LANES)
        cut = HEAD // 8
        first_ok, rest_ok = at.masks(u)
        zero = jnp.zeros((8, LANES), jnp.float32)
        first = jnp.where(first_ok, jnp.sum(sq[:cut], axis=0), zero)
        rest = jnp.where(rest_ok, jnp.sum(sq[cut:], axis=0), zero)
        acc[k] += first + rest

    def hold(buf, u, value):
        buf[pl.ds(u * TILE, TILE), :] = value

    def held(buf, u):
        return buf[pl.ds(u * TILE, TILE), :].T

    def rows_a(at, u):
        hold(ya, u, five(lambda k: nat(xs, at, u, k, True), 1))

    def turn_a(at, u):
        put(y1t, at, u, held(ya, u))

    def cols_b(at, u):
        put(c1t, at, u, columns(y1t, at, u, 1) * (1.0 / 256))

    def turn_b(at, u):
        value = c1t[pl.ds(at.turned_at(u) + SIDE, LANES), :].T
        nat_put(c1, at, u, value)
        plane = nat(xs, at, u, 0, True) - value
        out_put(o1, at, u, plane)
        add_squares(0, at, u, plane)

    def cols_c(at, u):
        hold(zt, u, columns(c1t, at, u, 2))

    def turn_c(at, u):
        nat_put(z, at, u, held(zt, u))

    def rows_d(at, u):
        value = five(lambda k: nat(z, at, u, k), 2) * (1.0 / 256)
        nat_put(c2, at, u, value)
        plane = nat(c1, at, u) - value
        out_put(o2, at, u, plane)
        add_squares(1, at, u, plane)

    def rows_e(at, u):
        hold(ye, u, five(lambda k: nat(c2, at, u, k), 4))

    def turn_e(at, u):
        put(y3t, at, u, held(ye, u))

    def cols_f(at, u):
        hold(c3t, u, columns(y3t, at, u, 4) * (1.0 / 256))

    def turn_f(at, u):
        value = held(c3t, u)
        out_put(o4, at, u, value)
        plane = nat(c2, at, u) - value
        out_put(o3, at, u, plane)
        add_squares(2, at, u, plane)

    stages = dict(
        a=rows_a, A=turn_a, b=cols_b, B=turn_b, c=cols_c, C=turn_c, d=rows_d, e=rows_e, E=turn_e, f=cols_f, F=turn_f
    )

    def run(spans, within):
        def outer(p, carry):
            boundary(p, within)
            for lo, hi, names in spans:

                def inner(r, c, names=names):
                    m, ml = c
                    for name in reversed(names):
                        at = Place(name, p, r, m, ml)
                        for u in (0, 1):
                            stages[name](at, u)
                    m, ml = m + 2, ml + 2
                    return jnp.where(m >= ring, m - ring, m), jnp.where(ml >= long, ml - long, ml)

                carry = lax.fori_loop(lo, hi, inner, carry)
            return carry

        return outer

    acc[...] = jnp.zeros_like(acc)
    request(jnp.int32(1))
    build_side(0, jnp.int32(0))
    mirror_rows(jnp.int32(0))
    ends = {st: tiles * (strips + 2) + lag for st, lag in lags.items()}
    for st in "fF":
        ends[st] -= tiles
    starts = dict(lags, f=lags["f"] + tiles, F=lags["F"] + tiles)
    carry = (jnp.int32(0), jnp.int32(0))
    total = -(-ends["F"] // (2 * tiles))
    plan = []
    for p in range(total):
        spans = []
        for r in range(tiles):
            i = 2 * (tiles * p + r)
            names = "".join(st for st in STAGES if starts[st] - 1 <= i < ends[st])
            if spans and (spans[-1][2] == names or spans[-1][1] - spans[-1][0] < 2):
                names = "".join(st for st in STAGES if st in names or st in spans[-1][2])
                spans[-1] = (spans[-1][0], r + 1, names)
            elif names:
                spans.append((r, r + 1, names))
        oldest = 2 * p - 4 - max(-(-lags[st] // tiles) for _, _, st in outs)
        key = (spans, oldest >= 1, 2 * p + 3 <= strips)
        if plan and plan[-1][2] == key:
            plan[-1] = (plan[-1][0], p + 1, key)
        else:
            plan.append((p, p + 1, key))
    for lo, hi, key in plan:
        carry = lax.fori_loop(lo, hi, run(key[0], (lo, hi)), carry)
    for p in range(total, total + 4):
        boundary(jnp.int32(p), (p, p + 1))
    lane = lax.broadcasted_iota(jnp.int32, (1, LANES), 1)
    sums = jnp.zeros((1, LANES), jnp.float32)
    for k in range(3):
        sums = jnp.where(lane == k, jnp.sum(acc[k]), sums)
    squares[...] = jnp.broadcast_to(sums[None], squares.shape)


def transform(x, rims, sides, devices):
    rows, cols = x.shape
    strips = cols // LANES
    assert rows % TILE == 0 and cols % (2 * LANES) == 0
    tiles = (rows + HEAD + EDGE + TILE - 1) // TILE
    hbm = pl.BlockSpec(memory_space=pl.ANY)
    vmem = pl.BlockSpec(memory_space=pltpu.VMEM)
    big = jax.ShapeDtypeStruct((rows, cols), jnp.float32)
    natural = lambda n: pltpu.VMEM((n * tiles * TILE + 2 * PAD, LANES), jnp.float32)
    turned = pltpu.VMEM((RING * tiles * (LANES + 2 * SIDE), TILE), jnp.float32)
    held = pltpu.VMEM((2 * TILE, LANES), jnp.float32)
    out = pltpu.VMEM((LONG * tiles * TILE, LANES), jnp.float32)
    return pl.pallas_call(
        functools.partial(kernel, rows=rows, strips=strips),
        in_specs=[hbm, hbm, hbm] + [vmem] * 4,
        out_specs=[hbm, hbm, hbm, hbm, vmem],
        out_shape=[big, big, big, big, jax.ShapeDtypeStruct((devices, 1, LANES), jnp.float32)],
        scratch_shapes=[
            natural(LONG), turned, turned, natural(RING), natural(RING), natural(RING), turned, out, out, out, out,
            held, held, held, held,
            pltpu.VMEM((3, 8, LANES), jnp.float32),
            pltpu.VMEM((EDGE, rows + LANES), jnp.float32),
            pltpu.SemaphoreType.DMA((LONG, 3)),
            pltpu.SemaphoreType.DMA((4, LONG)),
        ],
        compiler_params=pltpu.CompilerParams(vmem_limit_bytes=58 * 1024 * 1024),
        name="starlet",
    )(x, *rims, *sides)


def edge_kernel(left, right, first, last):
    for at in range(0, left.shape[0], TILE):
        first[:, at : at + TILE] = left[at : at + TILE, :].T[:EDGE]
        last[:, at : at + TILE] = right[at : at + TILE, :].T[LANES - EDGE :]
    for ref in (first, last):
        ref[:, left.shape[0] :] = jnp.zeros((EDGE, LANES), jnp.float32)


def turned_edges(x):
    rows, cols = x.shape
    strip = lambda i: pl.BlockSpec((rows, LANES), lambda g: (0, i))
    out = pl.BlockSpec((EDGE, rows + LANES), lambda g: (0, 0))
    shape = jax.ShapeDtypeStruct((EDGE, rows + LANES), jnp.float32)
    return pl.pallas_call(
        edge_kernel,
        grid=(1,),
        in_specs=[strip(0), strip(cols // LANES - 1)],
        out_specs=[out, out],
        out_shape=[shape, shape],
        cost_estimate=pl.CostEstimate(flops=0, bytes_accessed=8 * rows * LANES, transcendentals=0),
        name="edges",
    )(x, x)


def neighbours(first, last, axis):
    count = lax.axis_size(axis)
    up = [(i, i + 1) for i in range(count - 1)]
    down = [(i + 1, i) for i in range(count - 1)]
    return lax.ppermute(last, axis, up), lax.ppermute(first, axis, down)


def on_device(cube):
    x = cube[0]
    rows, cols = x.shape
    devices = lax.axis_size("rows") * lax.axis_size("cols")
    first, last = turned_edges(x)
    above, below = neighbours(x[:EDGE], x[rows - EDGE :], "rows")

    def cornered(edge, a, b):
        both = jnp.concatenate([above[:, a:b].T, below[:, a:b].T], axis=1)
        both = jnp.pad(both, ((0, 0), (0, LANES - 2 * EDGE)))
        return lax.dynamic_update_slice(edge, both, (0, rows))

    first, last = cornered(first, 0, EDGE), cornered(last, cols - EDGE, cols)
    left, right = neighbours(first, last, "cols")
    w1, w2, w3, smooth, squares = transform(x, (above, below), (left, right, first, last), devices)
    sums = jnp.sum(lax.all_to_all(squares, ("rows", "cols"), 0, 0), axis=(0, 1))
    sigmas = jnp.sqrt(sums[:3] / float(devices * rows * cols) + 1e-06)[:, None]
    return w1[None], w2[None], w3[None], smooth[None], sigmas


def solution(mesh):
    whole = P(None, "rows", "cols")
    return jax.shard_map(
        on_device, mesh=mesh, in_specs=(whole,), out_specs=(whole, whole, whole, whole, P()), check_vma=False
    )
```

```python
import functools

import jax
import jax.numpy as jnp
from jax import lax
from jax.experimental import pallas as pl
from jax.experimental.pallas import tpu as pltpu
from jax.sharding import PartitionSpec as P

LANES = 128
TILE = 128
REACH = 14
EDGE = 16
HEAD = 24
PAD = 8
SIDE = 8
RING = 4
LONG = 6


def five(load, step):
    a, b, c, d, e = (load(k * step) for k in (-2, -1, 0, 1, 2))
    return (a + e) + 4.0 * (b + d) + 6.0 * c


STAGES = "aAbBcCdeEfF"


def stage_lags(tiles):
    even = lambda n: n + n % 2
    lags = dict(a=0)
    after = dict(A=0, b=tiles, B=0, c=tiles, C=0, d=1, e=1, E=0, f=tiles, F=0)
    source = dict(A="a", b="A", B="b", c="b", C="c", d="C", e="d", E="e", f="E", F="f")
    for st in STAGES[1:]:
        lags[st] = even(lags[source[st]] + after[st] + 2)
    return lags


def kernel(x, top, bottom, left, right, first, last, w1, w2, w3, smooth, squares, xs, y1t, c1t, c1, z, c2, y3t, o1, o2, o3, o4,
           ya, zt, ye, c3t, acc, edge, isem, osem, *, rows, strips):
    tiles = (rows + HEAD + EDGE + TILE - 1) // TILE
    tall = tiles * TILE
    lags = stage_lags(tiles)
    ring, long = RING * tiles, LONG * tiles
    outs = ((o1, w1, "B"), (o2, w2, "d"), (o3, w3, "F"), (o4, smooth, "F"))

    def slot_of(s):
        return lax.rem(s, LONG)

    def in_copies(s):
        slot = slot_of(s)
        base = pl.multiple_of(slot * tall + PAD, 8)
        cols = pl.ds(pl.multiple_of((s - 1) * LANES, LANES), LANES)
        return (
            pltpu.make_async_copy(x.at[:, cols], xs.at[pl.ds(base + HEAD, rows), :], isem.at[slot, 0]),
            pltpu.make_async_copy(top.at[:, cols], xs.at[pl.ds(base + HEAD - EDGE, EDGE), :], isem.at[slot, 1]),
            pltpu.make_async_copy(bottom.at[:, cols], xs.at[pl.ds(base + HEAD + rows, EDGE), :], isem.at[slot, 2]),
        )

    row_pos, col_pos = lax.axis_index("rows"), lax.axis_index("cols")
    row_ends = (row_pos == 0, row_pos == lax.axis_size("rows") - 1)
    col_ends = (col_pos == 0, col_pos == lax.axis_size("cols") - 1)

    def build_side(side, s):
        got, own = ((left, first), (right, last))[side]
        edge[...] = got[...]

        @pl.when(col_ends[side])
        def _():
            for k in range(1, EDGE):
                at = EDGE - k if side == 0 else k - 1
                edge[pl.ds(at, 1), :] = own[pl.ds(k if side == 0 else EDGE - 1 - k, 1), :]

        base = pl.multiple_of(slot_of(s) * tall + PAD + HEAD, 8)
        blank = jnp.zeros((LANES - EDGE, TILE), jnp.float32)

        def turn(part):
            return jnp.concatenate([blank, part] if side == 0 else [part, blank], axis=0).T

        for at in range(0, rows, TILE):
            xs[pl.ds(base + at, TILE), :] = turn(edge[:, at : at + TILE])
        ends = turn(edge[:, rows:])
        xs[pl.ds(base - EDGE, EDGE), :] = ends[:EDGE]
        xs[pl.ds(base + rows, EDGE), :] = ends[EDGE : 2 * EDGE]

    def mirror_rows(s):
        base = slot_of(s) * tall + PAD + HEAD

        @pl.when(row_ends[0])
        def _():
            for k in range(1, REACH + 1):
                xs[pl.ds(base - k, 1), :] = xs[pl.ds(base + k, 1), :]

        @pl.when(row_ends[1])
        def _():
            for k in range(1, REACH + 1):
                xs[pl.ds(base + rows - 1 + k, 1), :] = xs[pl.ds(base + rows - 1 - k, 1), :]

    def guarded(fn, p, span, ahead):
        lo, hi = 2 * span[0] + ahead, 2 * (span[1] - 1) + ahead
        s = 2 * p + ahead
        if lo >= 1 and hi <= strips:
            fn(s)
        elif hi >= 1 and lo <= strips:
            pl.when((s >= 1) & (s <= strips))(lambda: fn(s))

    def request(s):
        for c in in_copies(s):
            c.start()

    def receive(s):
        for c in in_copies(s):
            c.wait()
        mirror_rows(s)

    def out_copy(k, s):
        buf, dst, _ = outs[k]
        slot = slot_of(s)
        base = pl.multiple_of(slot * tall + HEAD, 8)
        cols = pl.ds(pl.multiple_of((s - 1) * LANES, LANES), LANES)
        return pltpu.make_async_copy(buf.at[pl.ds(base, rows), :], dst.at[:, cols], osem.at[k, slot])

    def boundary(p, span):
        for u in (2, 3):
            guarded(request, p, span, u)
        for u in (0, 1):
            guarded(receive, p, span, u)
        if span[0] <= strips // 2 < span[1]:

            @pl.when(p == strips // 2)
            def _():
                build_side(1, strips + 1)
                mirror_rows(strips + 1)

        for k, (_, _, st) in enumerate(outs):
            newest = -1 - -(-lags[st] // tiles)
            for ahead in (newest - 3, newest - 2):
                guarded(lambda s: out_copy(k, s).wait(), p, span, ahead)
            for ahead in (newest - 1, newest):
                guarded(lambda s: out_copy(k, s).start(), p, span, ahead)

    def wrap(i, n):
        return jnp.where(i < 0, i + n, i)

    class Place:
        def __init__(self, st, p, r, m, ml):
            lag = lags[st]
            self.short = wrap(m - lag % ring, ring)
            self.long = wrap(ml - lag % long, long)
            self.q = 2 * tiles * p + 2 * r - lag
            self.x = 2 * r + (-lag) % tiles

        def rows_at(self, u, buf_long=False):
            i = self.long if buf_long else self.short
            return pl.multiple_of(i * TILE, TILE) + u * TILE

        def turned_at(self, u, strip=0):
            if strip == 0:
                return pl.multiple_of(self.short * (LANES + 2 * SIDE), 8) + u * (LANES + 2 * SIDE)
            i = self.short + u + strip * tiles
            i = jnp.where(i >= ring, i - ring, i) if strip > 0 else wrap(i, ring)
            return pl.multiple_of(i * (LANES + 2 * SIDE), 8)

        def masks(self, u):
            q, rb = self.q + u, self.x + u
            for _ in range(3):
                rb = jnp.where(rb >= tiles, rb - tiles, rb)
            ok = (q >= tiles) & (q < tiles * (strips + 1))
            return ok & (rb > 0), ok & (rb < tiles - 1)

    def nat(buf, at, u, shift=0, is_long=False):
        return buf[pl.ds(at.rows_at(u, is_long) + PAD + shift, TILE), :]

    def nat_put(buf, at, u, value):
        buf[pl.ds(at.rows_at(u) + PAD, TILE), :] = value

    def out_put(buf, at, u, value):
        buf[pl.ds(at.rows_at(u, True), TILE), :] = value

    def put(buf, at, u, value):
        buf[pl.ds(at.turned_at(u) + SIDE, LANES), :] = value
        buf[pl.ds(at.turned_at(u, 1), SIDE), :] = value[LANES - SIDE :]
        buf[pl.ds(at.turned_at(u, -1) + SIDE + LANES, SIDE), :] = value[:SIDE]

    def columns(buf, at, u, step):
        return five(lambda k: buf[pl.ds(at.turned_at(u) + SIDE + k, LANES), :], step)

    def add_squares(k, at, u, plane):
        sq = (plane * plane).reshape(TILE // 8, 8, LANES)
        cut = HEAD // 8
        first_ok, rest_ok = at.masks(u)
        zero = jnp.zeros((8, LANES), jnp.float32)
        first = jnp.where(first_ok, jnp.sum(sq[:cut], axis=0), zero)
        rest = jnp.where(rest_ok, jnp.sum(sq[cut:], axis=0), zero)
        acc[k] += first + rest

    def hold(buf, u, value):
        buf[pl.ds(u * TILE, TILE), :] = value

    def held(buf, u):
        return buf[pl.ds(u * TILE, TILE), :].T

    def rows_a(at, u):
        hold(ya, u, five(lambda k: nat(xs, at, u, k, True), 1))

    def turn_a(at, u):
        put(y1t, at, u, held(ya, u))

    def cols_b(at, u):
        put(c1t, at, u, columns(y1t, at, u, 1) * (1.0 / 256))

    def turn_b(at, u):
        value = c1t[pl.ds(at.turned_at(u) + SIDE, LANES), :].T
        nat_put(c1, at, u, value)
        plane = nat(xs, at, u, 0, True) - value
        out_put(o1, at, u, plane)
        add_squares(0, at, u, plane)

    def cols_c(at, u):
        hold(zt, u, columns(c1t, at, u, 2))

    def turn_c(at, u):
        nat_put(z, at, u, held(zt, u))

    def rows_d(at, u):
        value = five(lambda k: nat(z, at, u, k), 2) * (1.0 / 256)
        nat_put(c2, at, u, value)
        plane = nat(c1, at, u) - value
        out_put(o2, at, u, plane)
        add_squares(1, at, u, plane)

    def rows_e(at, u):
        hold(ye, u, five(lambda k: nat(c2, at, u, k), 4))

    def turn_e(at, u):
        put(y3t, at, u, held(ye, u))

    def cols_f(at, u):
        hold(c3t, u, columns(y3t, at, u, 4) * (1.0 / 256))

    def turn_f(at, u):
        value = held(c3t, u)
        out_put(o4, at, u, value)
        plane = nat(c2, at, u) - value
        out_put(o3, at, u, plane)
        add_squares(2, at, u, plane)

    stages = dict(
        a=rows_a, A=turn_a, b=cols_b, B=turn_b, c=cols_c, C=turn_c, d=rows_d, e=rows_e, E=turn_e, f=cols_f, F=turn_f
    )

    def run(spans, within):
        def outer(p, carry):
            boundary(p, within)
            for lo, hi, names in spans:

                def inner(r, c, names=names):
                    m, ml = c
                    places = {name: Place(name, p, r, m, ml) for name in names}
                    for u in (0, 1):
                        for name in reversed(names):
                            stages[name](places[name], u)
                    m, ml = m + 2, ml + 2
                    return jnp.where(m >= ring, m - ring, m), jnp.where(ml >= long, ml - long, ml)

                carry = lax.fori_loop(lo, hi, inner, carry)
            return carry

        return outer

    acc[...] = jnp.zeros_like(acc)
    request(jnp.int32(1))
    build_side(0, jnp.int32(0))
    mirror_rows(jnp.int32(0))
    ends = {st: tiles * (strips + 2) + lag for st, lag in lags.items()}
    for st in "fF":
        ends[st] -= tiles
    starts = dict(lags, f=lags["f"] + tiles, F=lags["F"] + tiles)
    carry = (jnp.int32(0), jnp.int32(0))
    total = -(-ends["F"] // (2 * tiles))
    plan = []
    for p in range(total):
        spans = []
        for r in range(tiles):
            i = 2 * (tiles * p + r)
            names = "".join(st for st in STAGES if starts[st] - 1 <= i < ends[st])
            if spans and (spans[-1][2] == names or spans[-1][1] - spans[-1][0] < 2):
                names = "".join(st for st in STAGES if st in names or st in spans[-1][2])
                spans[-1] = (spans[-1][0], r + 1, names)
            elif names:
                spans.append((r, r + 1, names))
        oldest = 2 * p - 4 - max(-(-lags[st] // tiles) for _, _, st in outs)
        key = (spans, oldest >= 1, 2 * p + 3 <= strips)
        if plan and plan[-1][2] == key:
            plan[-1] = (plan[-1][0], p + 1, key)
        else:
            plan.append((p, p + 1, key))
    for lo, hi, key in plan:
        carry = lax.fori_loop(lo, hi, run(key[0], (lo, hi)), carry)
    for p in range(total, total + 4):
        boundary(jnp.int32(p), (p, p + 1))
    lane = lax.broadcasted_iota(jnp.int32, (1, LANES), 1)
    sums = jnp.zeros((1, LANES), jnp.float32)
    for k in range(3):
        sums = jnp.where(lane == k, jnp.sum(acc[k]), sums)
    squares[...] = jnp.broadcast_to(sums[None], squares.shape)


def transform(x, rims, sides, devices):
    rows, cols = x.shape
    strips = cols // LANES
    assert rows % TILE == 0 and cols % (2 * LANES) == 0
    tiles = (rows + HEAD + EDGE + TILE - 1) // TILE
    hbm = pl.BlockSpec(memory_space=pl.ANY)
    vmem = pl.BlockSpec(memory_space=pltpu.VMEM)
    big = jax.ShapeDtypeStruct((rows, cols), jnp.float32)
    natural = lambda n: pltpu.VMEM((n * tiles * TILE + 2 * PAD, LANES), jnp.float32)
    turned = pltpu.VMEM((RING * tiles * (LANES + 2 * SIDE), TILE), jnp.float32)
    held = pltpu.VMEM((2 * TILE, LANES), jnp.float32)
    out = pltpu.VMEM((LONG * tiles * TILE, LANES), jnp.float32)
    return pl.pallas_call(
        functools.partial(kernel, rows=rows, strips=strips),
        in_specs=[hbm, hbm, hbm] + [vmem] * 4,
        out_specs=[hbm, hbm, hbm, hbm, vmem],
        out_shape=[big, big, big, big, jax.ShapeDtypeStruct((devices, 1, LANES), jnp.float32)],
        scratch_shapes=[
            natural(LONG), turned, turned, natural(RING), natural(RING), natural(RING), turned, out, out, out, out,
            held, held, held, held,
            pltpu.VMEM((3, 8, LANES), jnp.float32),
            pltpu.VMEM((EDGE, rows + LANES), jnp.float32),
            pltpu.SemaphoreType.DMA((LONG, 3)),
            pltpu.SemaphoreType.DMA((4, LONG)),
        ],
        compiler_params=pltpu.CompilerParams(vmem_limit_bytes=58 * 1024 * 1024),
        name="starlet",
    )(x, *rims, *sides)


def edge_kernel(left, right, first, last):
    for at in range(0, left.shape[0], TILE):
        first[:, at : at + TILE] = left[at : at + TILE, :].T[:EDGE]
        last[:, at : at + TILE] = right[at : at + TILE, :].T[LANES - EDGE :]
    for ref in (first, last):
        ref[:, left.shape[0] :] = jnp.zeros((EDGE, LANES), jnp.float32)


def turned_edges(x):
    rows, cols = x.shape
    strip = lambda i: pl.BlockSpec((rows, LANES), lambda g: (0, i))
    out = pl.BlockSpec((EDGE, rows + LANES), lambda g: (0, 0))
    shape = jax.ShapeDtypeStruct((EDGE, rows + LANES), jnp.float32)
    return pl.pallas_call(
        edge_kernel,
        grid=(1,),
        in_specs=[strip(0), strip(cols // LANES - 1)],
        out_specs=[out, out],
        out_shape=[shape, shape],
        cost_estimate=pl.CostEstimate(flops=0, bytes_accessed=8 * rows * LANES, transcendentals=0),
        name="edges",
    )(x, x)


def neighbours(first, last, axis):
    count = lax.axis_size(axis)
    up = [(i, i + 1) for i in range(count - 1)]
    down = [(i + 1, i) for i in range(count - 1)]
    return lax.ppermute(last, axis, up), lax.ppermute(first, axis, down)


def on_device(cube):
    x = cube[0]
    rows, cols = x.shape
    devices = lax.axis_size("rows") * lax.axis_size("cols")
    first, last = turned_edges(x)
    above, below = neighbours(x[:EDGE], x[rows - EDGE :], "rows")

    def cornered(edge, a, b):
        both = jnp.concatenate([above[:, a:b].T, below[:, a:b].T], axis=1)
        both = jnp.pad(both, ((0, 0), (0, LANES - 2 * EDGE)))
        return lax.dynamic_update_slice(edge, both, (0, rows))

    first, last = cornered(first, 0, EDGE), cornered(last, cols - EDGE, cols)
    left, right = neighbours(first, last, "cols")
    w1, w2, w3, smooth, squares = transform(x, (above, below), (left, right, first, last), devices)
    sums = jnp.sum(lax.all_to_all(squares, ("rows", "cols"), 0, 0), axis=(0, 1))
    sigmas = jnp.sqrt(sums[:3] / float(devices * rows * cols) + 1e-06)[:, None]
    return w1[None], w2[None], w3[None], smooth[None], sigmas


def solution(mesh):
    whole = P(None, "rows", "cols")
    return jax.shard_map(
        on_device, mesh=mesh, in_specs=(whole,), out_specs=(whole, whole, whole, whole, P()), check_vma=False
    )
```
